128 devices in a mesh: keys: 32 (over y, z, core), heads: 4 (over x).
Axes of the slice: x: 4, y: 4, z: 4, core: 2. Of those that a mesh axis runs over, the one named last changes fastest.
Arguments:
- main_query: bfloat16 [512, 128, 576], P(None, 'heads'), may hold values from -60 to 60
- latent_keys: bfloat16 [16384, 576], P('keys'), may hold values from -5 to 5
- index_query: bfloat16 [512, 64, 128], P(None, 'heads'), may hold values from -60 to 60
- index_keys: bfloat16 [16384, 128], P('keys'), may hold values from -5 to 5
- index_weights: float32 [512, 64], P(None, 'heads'), may hold values from -10 to 10
- query_limit: int32 [512], replicated, may hold values from 1 to 16383, as said below
Outputs:
- grad_index_query: float32 [512, 64, 128], P('keys', 'heads')
- grad_index_weights: float32 [512, 64], P('keys', 'heads')
- grad_index_keys: float32 [16384, 128], P('keys')
The draws below stay inside these ranges and needn't reach their ends.
Inputs may be any that keep to these rules, and one draw needn't show every extreme that they name: `query_limit`: Non-decreasing over the rows; the first row's value is 1 and the last row's is 16383.
All inputs are finite; a program needn't handle non-finite values.
Results may differ from the reference program's by a relative error of at most 0.0025.
Values sent between devices are 32-bit elements; how exact they have to be, the bound alone decides.
A program may use at most 192 MiB of HBM per device.

```python
import jax
import jax.numpy as jnp
from jax import lax

H = 128
DL = 576
HI = 64
DI = 128
QUERIES = 512
KEYS = 16384


def normal_block(key, tag, shape):
    return jnp.clip(jax.random.normal(jax.random.fold_in(key, tag), shape, jnp.float32), -5.0, 5.0)


def draw_latent_keys(key, part):
    return normal_block(key, 11, (KEYS, DL)).astype(jnp.bfloat16)


def draw_index_keys(key, part):
    return normal_block(key, 12, (KEYS, DI)).astype(jnp.bfloat16)


def draw_main_query(key, part):
    base = normal_block(key, 21, (QUERIES, H, DL))
    return base.astype(jnp.bfloat16)


def draw_index_query(key, part):
    base = normal_block(key, 22, (QUERIES, HI, DI))
    return base.astype(jnp.bfloat16)


def draw_index_weights(key, part):
    base = jnp.clip(2.5 * jax.random.normal(jax.random.fold_in(key, 31), (QUERIES, HI), jnp.float32), -10.0, 10.0)
    return base


def draw_query_limit(key, part):
    values = jax.random.randint(jax.random.fold_in(key, 41), (QUERIES,), 1, KEYS, dtype=jnp.int32)
    values = jnp.sort(values)
    return values.at[0].set(1).at[QUERIES - 1].set(KEYS - 1)


def setup_inputs(seed: int = 0) -> dict:
    streams_of = jax.random.split(jax.random.key(seed), 7)
    main_query = draw_main_query(jax.random.fold_in(streams_of[6], 71), 0)
    latent_keys = draw_latent_keys(jax.random.fold_in(streams_of[6], 71), 0)
    index_query = draw_index_query(jax.random.fold_in(streams_of[6], 71), 0)
    index_keys = draw_index_keys(jax.random.fold_in(streams_of[6], 71), 0)
    index_weights = draw_index_weights(jax.random.fold_in(streams_of[6], 71), 0)
    query_limit = draw_query_limit(jax.random.fold_in(streams_of[6], 71), 0)
    return {"main_query": main_query, "latent_keys": latent_keys, "index_query": index_query, "index_keys": index_keys, "index_weights": index_weights, "query_limit": query_limit}


def reference(main_query, latent_keys, index_query, index_keys, index_weights, query_limit):
    key_positions = jnp.arange(KEYS, dtype=jnp.int32)
    visible = key_positions[None, :] <= query_limit[:, None]
    score_scale = 2.0 * DL ** -0.5
    index_scale = DI ** -0.5
    head_scale = HI ** -0.5

    def one_head(carry, head_index):
        query_rows = lax.dynamic_index_in_dim(main_query, head_index, 1, keepdims=False)
        scores = jnp.dot(query_rows, latent_keys.T, preferred_element_type=jnp.float32) * score_scale
        scores = jnp.where(visible, scores, -1e30)
        row_max = jnp.max(scores, axis=1, keepdims=True)
        expos = jnp.where(visible, jnp.exp(scores - row_max), 0.0)
        return carry + expos / jnp.sum(expos, axis=1, keepdims=True), None

    target = lax.scan(one_head, jnp.zeros((QUERIES, KEYS), jnp.float32), jnp.arange(H, dtype=jnp.int32))[0] / H

    def index_dots_of(head_index):
        query_rows = lax.dynamic_index_in_dim(index_query, head_index, 1, keepdims=False)
        return jnp.dot(query_rows, index_keys.T, preferred_element_type=jnp.float32) * index_scale

    def index_forward(carry, head_index):
        dots = index_dots_of(head_index)
        weight_col = lax.dynamic_index_in_dim(index_weights, head_index, 1, keepdims=False)
        return carry + weight_col[:, None] * jnp.maximum(dots, 0.0), None

    heads_range = jnp.arange(HI, dtype=jnp.int32)
    logits = head_scale * lax.scan(index_forward, jnp.zeros((QUERIES, KEYS), jnp.float32), heads_range)[0]
    logits = jnp.where(visible, logits, -1e30)
    logit_max = jnp.max(logits, axis=1, keepdims=True)
    expos = jnp.where(visible, jnp.exp(logits - logit_max), 0.0)
    index_probs = expos / jnp.sum(expos, axis=1, keepdims=True)
    logit_grad = (index_probs - target) * (query_limit + 1).astype(jnp.float32)[:, None]

    def index_backward(carry, head_index):
        dots = index_dots_of(head_index)
        weight_col = lax.dynamic_index_in_dim(index_weights, head_index, 1, keepdims=False)
        grad_tile = jnp.where(dots > 0, logit_grad * weight_col[:, None] * head_scale, 0.0).astype(jnp.bfloat16)
        query_grad = jnp.dot(grad_tile, index_keys, preferred_element_type=jnp.float32) * index_scale
        query_rows = lax.dynamic_index_in_dim(index_query, head_index, 1, keepdims=False)
        key_grad = jnp.dot(grad_tile.T, query_rows, preferred_element_type=jnp.float32)
        weight_grad = head_scale * jnp.sum(logit_grad * jnp.maximum(dots, 0.0), axis=1)
        return carry + key_grad, (query_grad, weight_grad)

    key_total, stacked = lax.scan(index_backward, jnp.zeros((KEYS, DI), jnp.float32), heads_range)
    grad_index_query = jnp.transpose(stacked[0], (1, 0, 2))
    grad_index_weights = stacked[1].T
    return grad_index_query, grad_index_weights, key_total * index_scale
```

```python
import functools

import jax
import jax.numpy as jnp
from jax import lax
from jax.experimental import pallas as pl
from jax.experimental.pallas import tpu as pltpu
from jax.sharding import PartitionSpec as P

H = 128
DL = 576
HI = 64
DI = 128
NK = 32
NX = 4
NY = 4
NZ = 4
C = 4
T = 128
S = 512
SQ = S // NX
HL = H // NX
JL = HI // NX
LOG2E = 1.4426950408889634
K2 = 2.0 * DL ** (-0.5) * LOG2E
IS = DI ** (-0.5)
HS = HI ** (-0.5)
NEG = -1e30
BIG = 3e38
MESH = pl.DeviceIdType.MESH
F32 = jnp.float32
BF16 = jnp.bfloat16


def twice(a):
    return jnp.concatenate([a, a], axis=1)


def kernel(
    q_hbm, k_ref, iq_ref, ik_ref, w_ref, lim_ref,
    oq_ref, ow_ref, ok_ref,
    qb, p_ref, s_ref, m_ref, cap_ref, ikt_ref, wj_ref, gj_ref,
    lo_ref, lr_ref, lq_ref, ls_ref, xr_ref, lk_ref, kr_ref, lf_ref,
    st_ref, sr_ref, rr_ref, gl_ref, cc_ref,
    tg_ref, tr_ref, lg_ref, gw_ref, ka_ref,
    qp_ref, pr_ref, qs_ref, zr_ref, ys_ref, yr_ref, kx_ref, ko_ref,
    qsem,
    lo_s, lo_r, xs_s, xs_r, kk_s, kk_r, ss_s, ss_r, gl_s, gl_r, tg_s, tg_r,
    lg_s, lg_r, pp_s, pp_r, zz_s, zz_r, yy_s, yy_r, kx_s, kx_r, ko_s, ko_r,
):
    k = lax.axis_index("keys")
    x = lax.axis_index("heads")
    core = lax.rem(k, 2)
    z = lax.rem(k // 2, NZ)
    y = k // (2 * NZ)
    myq = pl.multiple_of(x * SQ, SQ)

    def q_copy(c):
        return pltpu.make_async_copy(
            q_hbm.at[:, :, pl.ds(c * T, T)], qb.at[c % 2], qsem.at[c % 2]
        )

    def send(src, dst, ssem, rsem, kd, xd):
        pltpu.make_async_remote_copy(
            src_ref=src, dst_ref=dst, send_sem=ssem, recv_sem=rsem,
            device_id=(kd, xd), device_id_type=MESH,
        ).start()

    def wait(ref, sem):
        pltpu.make_async_copy(ref, ref, sem).wait()

    def to_keys(fn):
        def body(r, carry):
            fn(r, lax.rem(k + r, NK))
            return carry

        lax.fori_loop(1, NK, body, 0)

    def to_heads(fn):
        for r in range(1, NX):
            fn(r, lax.rem(x + r, NX))

    q_copy(0).start()
    barrier = pltpu.get_barrier_semaphore()
    to_keys(lambda r, o: pl.semaphore_signal(barrier, inc=1, device_id=(o, x), device_id_type=MESH))
    to_heads(lambda r, o: pl.semaphore_signal(barrier, inc=1, device_id=(k, o), device_id_type=MESH))

    pos = k * S + lax.broadcasted_iota(jnp.int32, (S, T), 0)
    for c in range(C):
        cap_ref[c] = jnp.where(pos <= lim_ref[0:1, c * T : (c + 1) * T], BIG, NEG)
    for j in range(JL):
        wj_ref[j] = w_ref[j : j + 1, :]
    ikt_ref[...] = ik_ref[...].astype(F32).T.astype(BF16)
    pl.semaphore_wait(barrier, NK - 1 + NX - 1)

    def index_dots(c, jj):
        pair = iq_ref[pl.ds(2 * jj, 2), c * T : (c + 1) * T, :].reshape(2 * T, DI)
        dots = lax.dot_general(
            ik_ref[...], pair, (((1,), (1,)), ((), ())), preferred_element_type=F32
        )
        row = jnp.concatenate(
            [wj_ref[2 * jj, :, c * T : (c + 1) * T], wj_ref[2 * jj + 1, :, c * T : (c + 1) * T]],
            axis=1,
        )
        return pair, dots, row

    def index_forward(c):
        lo_ref[c] = jnp.zeros((S, T), F32)

        def body(jj, carry):
            _, dots, row = index_dots(c, jj)
            term = jnp.maximum(dots, 0.0) * (row * (IS * HS))
            lo_ref[c] += term[:, :T] + term[:, T:]
            return carry

        lax.fori_loop(0, JL // 2, body, 0)
        to_heads(lambda r, o: send(
            lo_ref.at[c, pl.ds(pl.multiple_of(o * SQ, SQ), SQ)], lr_ref.at[c, r - 1],
            lo_s.at[c], lo_r.at[c], k, o))

    def scores(c):
        q_copy(c).wait()
        if c + 1 < C:
            q_copy(c + 1).start()
        slot = c % 2
        ps = c % 3

        def dots(i, u):
            h = 2 * i
            qt = jnp.concatenate([qb[slot, h], qb[slot, h + 1]], axis=1)
            s = jnp.dot(k_ref[...], qt, preferred_element_type=F32)
            s = jnp.minimum(s, twice(cap_ref[c]))
            s_ref[u] = s
            m = jnp.max(s, axis=0, keepdims=True)
            m_ref[u] = m
            st_ref[c, h, 0:1, :] = m[:, :T]
            st_ref[c, h + 1, 0:1, :] = m[:, T:]

        def soft(i, u):
            h = 2 * i
            p = jnp.exp2((s_ref[u] - m_ref[u]) * K2)
            l = jnp.sum(p, axis=0, keepdims=True)
            p_ref[ps, h] = p[:, :T]
            p_ref[ps, h + 1] = p[:, T:]
            st_ref[c, h, 1:2, :] = l[:, :T]
            st_ref[c, h + 1, 1:2, :] = l[:, T:]

        dots(0, 0)

        def body(i, carry):
            dots(2 * i + 1, 1)
            soft(2 * i, 0)
            dots(jnp.minimum(2 * i + 2, HL // 2 - 1), 0)
            soft(2 * i + 1, 1)
            return carry

        lax.fori_loop(0, HL // 4, body, 0)
        to_keys(lambda r, o: send(
            st_ref.at[c, o], sr_ref.at[c, r - 1], ss_s.at[c], ss_r.at[c], o, x))

    def combine(c):
        wait(sr_ref.at[c], ss_r.at[c])
        own = st_ref[c, k]
        ms = sr_ref[c, :, 0, :]
        sums = sr_ref[c, :, 1, :]
        m = jnp.maximum(own[0:1], jnp.max(ms, axis=0, keepdims=True))
        total = own[1:2] * jnp.exp2((own[0:1] - m) * K2) + jnp.sum(
            sums * jnp.exp2((ms - m) * K2), axis=0, keepdims=True
        )
        rr_ref[c, 0:1, :] = m
        rr_ref[c, 1:2, :] = 1.0 / (total * H)
        gl_ref[c, k] = rr_ref[c]
        to_keys(lambda r, o: send(rr_ref.at[c], gl_ref.at[c, k], gl_s.at[c], gl_r.at[c], o, x))

    def logit_stats():
        for c in range(C):
            wait(lr_ref.at[c], lo_r.at[c])
            v = lo_ref[c, pl.ds(myq, SQ), :] + lr_ref[c, 0] + lr_ref[c, 1] + lr_ref[c, 2]
            v = jnp.minimum(v, cap_ref[c, pl.ds(myq, SQ), :])
            lq_ref[c] = v
            m = jnp.max(v, axis=0, keepdims=True)
            ls_ref[c, 0:1, :] = m
            ls_ref[c, 1:2, :] = jnp.sum(jnp.exp(v - m), axis=0, keepdims=True)
        to_heads(lambda r, o: send(ls_ref, xr_ref.at[r - 1], xs_s, xs_r, k, o))

    def logit_stats_heads():
        wait(xr_ref, xs_r)
        for c in range(C):
            ms = [ls_ref[c, 0:1, :]] + [xr_ref[r, c, 0:1, :] for r in range(NX - 1)]
            ts = [ls_ref[c, 1:2, :]] + [xr_ref[r, c, 1:2, :] for r in range(NX - 1)]
            m = functools.reduce(jnp.maximum, ms)
            lk_ref[c, 0:1, :] = m
            lk_ref[c, 1:2, :] = sum(t * jnp.exp(a - m) for a, t in zip(ms, ts))
        to_keys(lambda r, o: send(lk_ref, kr_ref.at[r - 1], kk_s, kk_r, o, x))

    def logit_stats_keys():
        wait(kr_ref, kk_r)
        for c in range(C):
            own_m, own_t = lk_ref[c, 0:1, :], lk_ref[c, 1:2, :]
            ms = kr_ref[:, c, 0, :]
            ts = kr_ref[:, c, 1, :]
            m = jnp.maximum(own_m, jnp.max(ms, axis=0, keepdims=True))
            lf_ref[c, 0:1, :] = m
            lf_ref[c, 1:2, :] = own_t * jnp.exp(own_m - m) + jnp.sum(
                ts * jnp.exp(ms - m), axis=0, keepdims=True
            )

    def target(c):
        wait(gl_ref.at[c, pl.ds(0, NK - 1)], gl_r.at[c])
        cc_ref[...] = jnp.exp2((st_ref[c, :, 0, :] - gl_ref[c, :, 0, :]) * K2) * gl_ref[c, :, 1, :]
        ps = c % 3
        rows = 64

        def body(b, carry):
            at = pl.ds(pl.multiple_of(b * rows, rows), rows)
            acc = p_ref[ps, 0, at, :] * cc_ref[0:1, :]
            for h in range(1, HL):
                acc += p_ref[ps, h, at, :] * cc_ref[h : h + 1, :]
            tg_ref[c, at, :] = acc
            return carry

        lax.fori_loop(0, S // rows, body, 0)
        to_heads(lambda r, o: send(
            tg_ref.at[c, pl.ds(pl.multiple_of(o * SQ, SQ), SQ)], tr_ref.at[c, r - 1],
            tg_s.at[c], tg_r.at[c], k, o))

    def logit_grad(c):
        wait(tr_ref.at[c], tg_r.at[c])
        t = tg_ref[c, pl.ds(myq, SQ), :] + tr_ref[c, 0] + tr_ref[c, 1] + tr_ref[c, 2]
        v = lq_ref[c]
        probs = jnp.where(
            cap_ref[c, pl.ds(myq, SQ), :] > 0, jnp.exp(v - lf_ref[c, 0:1, :]), 0.0
        ) / lf_ref[c, 1:2, :]
        span = (lim_ref[0:1, c * T : (c + 1) * T] + 1).astype(F32)
        lg_ref[c, pl.ds(myq, SQ), :] = (probs - t) * span
        to_heads(lambda r, o: send(
            lg_ref.at[c, pl.ds(myq, SQ)], lg_ref.at[c, pl.ds(myq, SQ)],
            lg_s.at[c], lg_r.at[c], k, o))

    def grads(c):
        wait(tr_ref.at[c], lg_r.at[c])

        def body(jj, carry):
            pair, dots, row = index_dots(c, jj)
            lg = twice(lg_ref[c])
            gw = jnp.sum(lg * jnp.maximum(dots, 0.0), axis=0, keepdims=True) * (IS * HS)
            gj_ref[2 * jj] = gw[:, :T]
            gj_ref[2 * jj + 1] = gw[:, T:]
            g = jnp.where(dots > 0, lg * (row * HS), 0.0).astype(BF16)
            qpt = jnp.dot(ikt_ref[...], g, preferred_element_type=F32)
            qp = qpt.T * IS
            for u in range(2):
                for zz in range(NZ):
                    for cr in range(2):
                        at = u * T + (zz * 2 + cr) * 16
                        qp_ref[c, cr, zz, 2 * jj + u] = qp[at : at + 16]
            part = jnp.dot(g, pair, preferred_element_type=F32)
            ka_ref[...] += part
            return carry

        lax.fori_loop(0, JL // 2, body, 0)
        for j in range(JL):
            gw_ref[j : j + 1, :] = gj_ref[j]
        gwt = gw_ref[...].T
        for zz in range(NZ):
            for cr in range(2):
                at = (zz * 2 + cr) * 16
                qp_ref[c, cr, zz, JL] = gwt[at : at + 16]
        send(qp_ref.at[c, 1 - core], pr_ref.at[c], pp_s.at[c], pp_r.at[c], k + 1 - 2 * core, x)

    def pair_sum(c):
        wait(pr_ref.at[c], pp_r.at[c])
        for zz in range(NZ):
            qs_ref[c, zz] = qp_ref[c, core, zz] + pr_ref[c, zz]
        for dz in range(1, NZ):
            zd = lax.rem(z + dz, NZ)
            send(qs_ref.at[c, zd], zr_ref.at[c, dz - 1], zz_s.at[c], zz_r.at[c], (y * NZ + zd) * 2 + core, x)

    def plane_sum(c):
        wait(zr_ref.at[c], zz_r.at[c])
        ys_ref[c] = qs_ref[c, z] + zr_ref[c, 0] + zr_ref[c, 1] + zr_ref[c, 2]
        slot = lax.rem(y - c + NY - 1, NY)

        @pl.when(y != c)
        def _():
            send(ys_ref.at[c], yr_ref.at[slot], yy_s.at[c], yy_r, (c * NZ + z) * 2 + core, x)

    def key_send():
        to_heads(lambda r, o: send(
            ka_ref.at[pl.ds(pl.multiple_of(o * SQ, SQ), SQ)], kx_ref.at[r - 1], kx_s, kx_r, k, o))

    def key_sum():
        wait(kx_ref, kx_r)
        ko_ref[pl.ds(myq, SQ), :] = (
            ka_ref[pl.ds(myq, SQ), :] + kx_ref[0] + kx_ref[1] + kx_ref[2]
        ) * IS
        to_heads(lambda r, o: send(
            ko_ref.at[pl.ds(myq, SQ)], ko_ref.at[pl.ds(myq, SQ)], ko_s, ko_r, k, o))

    gw_ref[...] = jnp.zeros_like(gw_ref)
    ka_ref[...] = jnp.zeros_like(ka_ref)
    for c in range(C):
        index_forward(c)
    scores(0)
    logit_stats()
    scores(1)
    combine(0)
    logit_stats_heads()
    scores(2)
    combine(1)
    target(0)
    logit_stats_keys()
    scores(3)
    combine(2)
    logit_grad(0)
    target(1)
    grads(0)
    combine(3)
    logit_grad(1)
    target(2)
    pair_sum(0)
    grads(1)
    logit_grad(2)
    target(3)
    plane_sum(0)
    pair_sum(1)
    grads(2)
    logit_grad(3)
    plane_sum(1)
    pair_sum(2)
    grads(3)
    key_send()
    plane_sum(2)
    pair_sum(3)
    key_sum()
    plane_sum(3)
    wait(yr_ref, yy_r)
    mine = ys_ref[y] + yr_ref[0] + yr_ref[1] + yr_ref[2]
    oq_ref[...] = mine[:JL]
    ow_ref[...] = mine[JL]
    wait(kx_ref, ko_r)
    ok_ref[...] = ko_ref[...]

    wait(xr_ref, xs_s)
    wait(kr_ref, kk_s)
    wait(kx_ref, kx_s)
    wait(kx_ref, ko_s)
    for c in range(C):
        wait(lr_ref.at[c], lo_s.at[c])
        wait(sr_ref.at[c], ss_s.at[c])
        wait(sr_ref.at[c], gl_s.at[c])
        wait(tr_ref.at[c], tg_s.at[c])
        wait(tr_ref.at[c], lg_s.at[c])
        wait(pr_ref.at[c], pp_s.at[c])
        wait(zr_ref.at[c], zz_s.at[c])

        @pl.when(y != c)
        def _():
            wait(ys_ref.at[c], yy_s.at[c])


def per_device(main_query, latent_keys, index_query, index_keys, index_weights, query_limit):
    vm = pl.BlockSpec(memory_space=pltpu.VMEM)
    dma = pltpu.SemaphoreType.DMA
    oq, ow, ok = pl.pallas_call(
        kernel,
        out_shape=(
            jax.ShapeDtypeStruct((JL, 16, DI), F32),
            jax.ShapeDtypeStruct((16, DI), F32),
            jax.ShapeDtypeStruct((S, DI), F32),
        ),
        in_specs=[pl.BlockSpec(memory_space=pl.ANY)] + [vm] * 5,
        out_specs=(vm, vm, vm),
        scratch_shapes=[
            pltpu.VMEM((2, HL, DL, T), BF16),
            pltpu.VMEM((3, HL, S, T), F32),
            pltpu.VMEM((2, S, 2 * T), F32),
            pltpu.VMEM((2, 1, 2 * T), F32),
            pltpu.VMEM((C, S, T), F32),
            pltpu.VMEM((DI, S), BF16),
            pltpu.VMEM((JL, 1, C * T), F32),
            pltpu.VMEM((JL, 1, T), F32),
            pltpu.VMEM((C, S, T), F32),
            pltpu.VMEM((C, NX - 1, SQ, T), F32),
            pltpu.VMEM((C, SQ, T), F32),
            pltpu.VMEM((C, 2, T), F32),
            pltpu.VMEM((NX - 1, C, 2, T), F32),
            pltpu.VMEM((C, 2, T), F32),
            pltpu.VMEM((NK - 1, C, 2, T), F32),
            pltpu.VMEM((C, 2, T), F32),
            pltpu.VMEM((C, HL, 2, T), F32),
            pltpu.VMEM((C, NK - 1, 2, T), F32),
            pltpu.VMEM((C, 2, T), F32),
            pltpu.VMEM((C, HL, 2, T), F32),
            pltpu.VMEM((HL, T), F32),
            pltpu.VMEM((C, S, T), F32),
            pltpu.VMEM((C, NX - 1, SQ, T), F32),
            pltpu.VMEM((C, S, T), F32),
            pltpu.VMEM((DI, T), F32),
            pltpu.VMEM((S, DI), F32),
            pltpu.VMEM((C, 2, NZ, JL + 1, 16, DI), F32),
            pltpu.VMEM((C, NZ, JL + 1, 16, DI), F32),
            pltpu.VMEM((C, NZ, JL + 1, 16, DI), F32),
            pltpu.VMEM((C, NZ - 1, JL + 1, 16, DI), F32),
            pltpu.VMEM((C, JL + 1, 16, DI), F32),
            pltpu.VMEM((NY - 1, JL + 1, 16, DI), F32),
            pltpu.VMEM((NX - 1, SQ, DI), F32),
            pltpu.VMEM((S, DI), F32),
            dma((2,)),
            dma((C,)), dma((C,)), dma, dma, dma, dma, dma((C,)), dma((C,)), dma((C,)), dma((C,)),
            dma((C,)), dma((C,)), dma((C,)), dma((C,)), dma((C,)), dma((C,)), dma((C,)), dma((C,)),
            dma((C,)), dma, dma, dma, dma, dma,
        ],
        compiler_params=pltpu.CompilerParams(
            collective_id=0, has_side_effects=True, vmem_limit_bytes=67043328
        ),
    )(
        jnp.transpose(main_query, (1, 2, 0)),
        latent_keys,
        jnp.transpose(index_query, (1, 0, 2)),
        index_keys,
        index_weights.T,
        query_limit.reshape(1, -1),
    )
    return jnp.transpose(oq, (1, 0, 2)), ow[:, :JL], ok


def solution(mesh):
    in_specs = (
        P(None, "heads", None),
        P("keys", None),
        P(None, "heads", None),
        P("keys", None),
        P(None, "heads"),
        P(),
    )
    out_specs = (P("keys", "heads", None), P("keys", "heads"), P("keys", None))
    return jax.shard_map(
        per_device, mesh=mesh, in_specs=in_specs, out_specs=out_specs, check_vma=False
    )
```

```python
import functools

import jax
import jax.numpy as jnp
from jax import lax
from jax.experimental import pallas as pl
from jax.experimental.pallas import tpu as pltpu
from jax.sharding import PartitionSpec as P

H = 128
DL = 576
HI = 64
DI = 128
NK = 32
NX = 4
NY = 4
NZ = 4
C = 4
T = 128
S = 512
SQ = S // NX
HL = H // NX
JL = HI // NX
LOG2E = 1.4426950408889634
K2 = 2.0 * DL ** (-0.5) * LOG2E
IS = DI ** (-0.5)
HS = HI ** (-0.5)
NEG = -1e30
BIG = 3e38
MESH = pl.DeviceIdType.MESH
F32 = jnp.float32
BF16 = jnp.bfloat16


def twice(a):
    return jnp.concatenate([a, a], axis=1)


def kernel(
    q_hbm, kt_hbm, iq_hbm, ik_hbm, w_ref, lim_ref,
    oq_ref, ow_ref, ok_ref,
    qb, p_ref, s_ref, m_ref, cap_ref, ikt_ref, wj_ref, gj_ref,
    kt_ref, k_ref, iqr_ref, tmp_ref, iq_ref, ik_ref, ga_ref, gb_ref,
    lo_ref, lr_ref, lq_ref, ls_ref, xr_ref, lk_ref, kr_ref, lf_ref,
    st_ref, sr_ref, rr_ref, gl_ref, cc_ref,
    tg_ref, tr_ref, lg_ref, gw_ref, ka_ref,
    qp_ref, pr_ref, qs_ref, zr_ref, ys_ref, yr_ref, kx_ref, ko_ref,
    qsem, isem,
    lo_s, lo_r, xs_s, xs_r, kk_s, kk_r, ss_s, ss_r, gl_s, gl_r, tg_s, tg_r,
    lg_s, lg_r, pp_s, pp_r, zz_s, zz_r, yy_s, yy_r, kx_s, kx_r, ko_s, ko_r,
):
    k = lax.axis_index("keys")
    x = lax.axis_index("heads")
    core = lax.rem(k, 2)
    z = lax.rem(k // 2, NZ)
    y = k // (2 * NZ)
    myq = pl.multiple_of(x * SQ, SQ)

    def q_copy(c):
        return pltpu.make_async_copy(
            q_hbm.at[:, :, pl.ds(c * T, T)], qb.at[c % 2], qsem.at[c % 2]
        )

    def send(src, dst, ssem, rsem, kd, xd):
        pltpu.make_async_remote_copy(
            src_ref=src, dst_ref=dst, send_sem=ssem, recv_sem=rsem,
            device_id=(kd, xd), device_id_type=MESH,
        ).start()

    def wait(ref, sem):
        pltpu.make_async_copy(ref, ref, sem).wait()

    def to_keys(fn):
        def body(r, carry):
            fn(r, lax.rem(k + r, NK))
            return carry

        lax.fori_loop(1, NK, body, 0)

    def to_heads(fn):
        for r in range(1, NX):
            fn(r, lax.rem(x + r, NX))

    loads = [
        pltpu.make_async_copy(a, b, isem.at[n])
        for n, (a, b) in enumerate(((iq_hbm, iqr_ref), (ik_hbm, ik_ref), (kt_hbm, kt_ref)))
    ]
    for load in loads:
        load.start()
    q_copy(0).start()
    barrier = pltpu.get_barrier_semaphore()
    to_keys(lambda r, o: pl.semaphore_signal(barrier, inc=1, device_id=(o, x), device_id_type=MESH))
    to_heads(lambda r, o: pl.semaphore_signal(barrier, inc=1, device_id=(k, o), device_id_type=MESH))

    pos = k * S + lax.broadcasted_iota(jnp.int32, (S, T), 0)
    for c in range(C):
        cap_ref[c] = jnp.where(pos <= lim_ref[0:1, c * T : (c + 1) * T], BIG, NEG)
    for j in range(JL):
        wj_ref[j] = w_ref[j : j + 1, :]
    loads[1].wait()
    ikt_ref[...] = ik_ref[...].astype(F32).T.astype(BF16)
    loads[0].wait()
    for c in range(C):
        tmp_ref[...] = iqr_ref[c * T : (c + 1) * T].astype(F32).reshape(T * JL, DI)
        for j in range(JL):
            iq_ref[j, c * T : (c + 1) * T] = tmp_ref[pl.ds(j, T, stride=JL), :].astype(BF16)

    def rows_of(c, jj):
        return jnp.concatenate(
            [wj_ref[2 * jj, :, c * T : (c + 1) * T], wj_ref[2 * jj + 1, :, c * T : (c + 1) * T]],
            axis=1,
        )

    def index_dots(c, jj, u):
        pair = iq_ref[pl.ds(2 * jj, 2), c * T : (c + 1) * T, :].reshape(2 * T, DI)
        s_ref[u] = lax.dot_general(
            ik_ref[...], pair, (((1,), (1,)), ((), ())), preferred_element_type=F32
        )

    def index_forward(c):
        lo_ref[c] = jnp.zeros((S, T), F32)

        def add(jj, u):
            total = None
            for v in range(2):
                row = rows_of(c, jj + v) * (IS * HS)
                term = jnp.maximum(s_ref[u + v], 0.0) * row
                part = term[:, :T] + term[:, T:]
                total = part if total is None else total + part
            lo_ref[c] += total

        def two(jj, u):
            index_dots(c, jj, u)
            index_dots(c, jj + 1, u + 1)

        two(0, 0)

        def body(i, carry):
            two(4 * i + 2, 2)
            add(4 * i, 0)
            two(jnp.minimum(4 * i + 4, JL // 2 - 2), 0)
            add(4 * i + 2, 2)
            return carry

        lax.fori_loop(0, JL // 8, body, 0)
        if c == 0:
            pl.semaphore_wait(barrier, NK - 1 + NX - 1)
        to_heads(lambda r, o: send(
            lo_ref.at[c, pl.ds(pl.multiple_of(o * SQ, SQ), SQ)], lr_ref.at[c, r - 1],
            lo_s.at[c], lo_r.at[c], k, o))

    def scores(c):
        q_copy(c).wait()
        if c == 0:
            loads[2].wait()
            for b in range(S // 128):
                k_ref[b * 128 : (b + 1) * 128, :] = (
                    kt_ref[:, b * 128 : (b + 1) * 128].astype(F32).T.astype(BF16)
                )
        if c + 1 < C:
            q_copy(c + 1).start()
        slot = c % 2
        ps = c % 3

        def dots(i, u):
            h = 2 * i
            qt = jnp.concatenate([qb[slot, h], qb[slot, h + 1]], axis=1)
            s = jnp.dot(k_ref[...], qt, preferred_element_type=F32)
            s = jnp.minimum(s, twice(cap_ref[c]))
            s_ref[u] = s
            m = jnp.max(s, axis=0, keepdims=True)
            m_ref[u] = m
            st_ref[c, h, 0:1, :] = m[:, :T]
            st_ref[c, h + 1, 0:1, :] = m[:, T:]

        def soft(i, u):
            h = 2 * i
            p = jnp.exp2((s_ref[u] - m_ref[u]) * K2)
            l = jnp.sum(p, axis=0, keepdims=True)
            p_ref[ps, h] = p[:, :T]
            p_ref[ps, h + 1] = p[:, T:]
            st_ref[c, h, 1:2, :] = l[:, :T]
            st_ref[c, h + 1, 1:2, :] = l[:, T:]

        dots(0, 0)

        def body(i, carry):
            dots(2 * i + 1, 1)
            soft(2 * i, 0)
            dots(jnp.minimum(2 * i + 2, HL // 2 - 1), 0)
            soft(2 * i + 1, 1)
            return carry

        lax.fori_loop(0, HL // 4, body, 0)
        to_keys(lambda r, o: send(
            st_ref.at[c, o], sr_ref.at[c, r - 1], ss_s.at[c], ss_r.at[c], o, x))

    def combine(c):
        wait(sr_ref.at[c], ss_r.at[c])
        own = st_ref[c, k]
        ms = sr_ref[c, :, 0, :]
        sums = sr_ref[c, :, 1, :]
        m = jnp.maximum(own[0:1], jnp.max(ms, axis=0, keepdims=True))
        total = own[1:2] * jnp.exp2((own[0:1] - m) * K2) + jnp.sum(
            sums * jnp.exp2((ms - m) * K2), axis=0, keepdims=True
        )
        rr_ref[c, 0:1, :] = m
        rr_ref[c, 1:2, :] = 1.0 / (total * H)
        gl_ref[c, k] = rr_ref[c]
        to_keys(lambda r, o: send(rr_ref.at[c], gl_ref.at[c, k], gl_s.at[c], gl_r.at[c], o, x))

    def logit_stats():
        for c in range(C):
            wait(lr_ref.at[c], lo_r.at[c])
            v = lo_ref[c, pl.ds(myq, SQ), :] + lr_ref[c, 0] + lr_ref[c, 1] + lr_ref[c, 2]
            v = jnp.minimum(v, cap_ref[c, pl.ds(myq, SQ), :])
            lq_ref[c] = v
            m = jnp.max(v, axis=0, keepdims=True)
            ls_ref[c, 0:1, :] = m
            ls_ref[c, 1:2, :] = jnp.sum(jnp.exp(v - m), axis=0, keepdims=True)
        to_heads(lambda r, o: send(ls_ref, xr_ref.at[r - 1], xs_s, xs_r, k, o))

    def logit_stats_heads():
        wait(xr_ref, xs_r)
        for c in range(C):
            ms = [ls_ref[c, 0:1, :]] + [xr_ref[r, c, 0:1, :] for r in range(NX - 1)]
            ts = [ls_ref[c, 1:2, :]] + [xr_ref[r, c, 1:2, :] for r in range(NX - 1)]
            m = functools.reduce(jnp.maximum, ms)
            lk_ref[c, 0:1, :] = m
            lk_ref[c, 1:2, :] = sum(t * jnp.exp(a - m) for a, t in zip(ms, ts))
        to_keys(lambda r, o: send(lk_ref, kr_ref.at[r - 1], kk_s, kk_r, o, x))

    def logit_stats_keys():
        wait(kr_ref, kk_r)
        for c in range(C):
            own_m, own_t = lk_ref[c, 0:1, :], lk_ref[c, 1:2, :]
            ms = kr_ref[:, c, 0, :]
            ts = kr_ref[:, c, 1, :]
            m = jnp.maximum(own_m, jnp.max(ms, axis=0, keepdims=True))
            lf_ref[c, 0:1, :] = m
            lf_ref[c, 1:2, :] = own_t * jnp.exp(own_m - m) + jnp.sum(
                ts * jnp.exp(ms - m), axis=0, keepdims=True
            )

    def target(c):
        wait(gl_ref.at[c, pl.ds(0, NK - 1)], gl_r.at[c])
        cc_ref[...] = jnp.exp2((st_ref[c, :, 0, :] - gl_ref[c, :, 0, :]) * K2) * gl_ref[c, :, 1, :]
        ps = c % 3
        rows = 64

        def body(b, carry):
            at = pl.ds(pl.multiple_of(b * rows, rows), rows)
            acc = p_ref[ps, 0, at, :] * cc_ref[0:1, :]
            for h in range(1, HL):
                acc += p_ref[ps, h, at, :] * cc_ref[h : h + 1, :]
            tg_ref[c, at, :] = acc
            return carry

        lax.fori_loop(0, S // rows, body, 0)
        to_heads(lambda r, o: send(
            tg_ref.at[c, pl.ds(pl.multiple_of(o * SQ, SQ), SQ)], tr_ref.at[c, r - 1],
            tg_s.at[c], tg_r.at[c], k, o))

    def logit_grad(c):
        wait(tr_ref.at[c], tg_r.at[c])
        t = tg_ref[c, pl.ds(myq, SQ), :] + tr_ref[c, 0] + tr_ref[c, 1] + tr_ref[c, 2]
        v = lq_ref[c]
        probs = jnp.where(
            cap_ref[c, pl.ds(myq, SQ), :] > 0, jnp.exp(v - lf_ref[c, 0:1, :]), 0.0
        ) / lf_ref[c, 1:2, :]
        span = (lim_ref[0:1, c * T : (c + 1) * T] + 1).astype(F32)
        lg_ref[c, pl.ds(myq, SQ), :] = (probs - t) * span
        to_heads(lambda r, o: send(
            lg_ref.at[c, pl.ds(myq, SQ)], lg_ref.at[c, pl.ds(myq, SQ)],
            lg_s.at[c], lg_r.at[c], k, o))

    def grads(c):
        wait(tr_ref.at[c], lg_r.at[c])

        def gate(jj, u, out, at):
            dots = s_ref[u]
            lg = twice(lg_ref[c])
            gw = jnp.sum(lg * jnp.maximum(dots, 0.0), axis=0, keepdims=True) * (IS * HS)
            gj_ref[2 * jj] = gw[:, :T]
            gj_ref[2 * jj + 1] = gw[:, T:]
            g = jnp.where(dots > 0, lg * (rows_of(c, jj) * HS), 0.0)
            out[:, at : at + 2 * T] = g.astype(BF16)

        def products(g_ref, j0):
            g = g_ref[...]
            four = iq_ref[pl.ds(j0, 4), c * T : (c + 1) * T, :].reshape(4 * T, DI)
            qpt = jnp.dot(ikt_ref[...], g, preferred_element_type=F32) * IS
            for u in range(4):
                qp = qpt[:, u * T : (u + 1) * T].T
                for zz in range(NZ):
                    for cr in range(2):
                        at = (zz * 2 + cr) * 16
                        qp_ref[c, cr, zz, j0 + u] = qp[at : at + 16]
            ka_ref[...] += jnp.dot(g, four, preferred_element_type=F32)

        gb_ref[...] = jnp.zeros_like(gb_ref)
        index_dots(c, 0, 0)

        def body(i, carry):
            products(gb_ref, jnp.maximum(8 * i - 4, 0))
            for u in range(4):
                index_dots(c, jnp.minimum(4 * i + u + 1, JL // 2 - 1), (u + 1) % 2)
                gate(4 * i + u, u % 2, ga_ref if u < 2 else gb_ref, (u % 2) * 2 * T)
                if u == 1:
                    products(ga_ref, 8 * i)
            return carry

        lax.fori_loop(0, JL // 8, body, 0)
        products(gb_ref, JL - 4)
        for j in range(JL):
            gw_ref[j : j + 1, :] = gj_ref[j]
        gwt = gw_ref[...].T
        for zz in range(NZ):
            for cr in range(2):
                at = (zz * 2 + cr) * 16
                qp_ref[c, cr, zz, JL] = gwt[at : at + 16]
        send(qp_ref.at[c, 1 - core], pr_ref.at[c], pp_s.at[c], pp_r.at[c], k + 1 - 2 * core, x)

    def pair_sum(c):
        wait(pr_ref.at[c], pp_r.at[c])
        for zz in range(NZ):
            qs_ref[c, zz] = qp_ref[c, core, zz] + pr_ref[c, zz]
        for dz in range(1, NZ):
            zd = lax.rem(z + dz, NZ)
            send(qs_ref.at[c, zd], zr_ref.at[c, dz - 1], zz_s.at[c], zz_r.at[c], (y * NZ + zd) * 2 + core, x)

    def plane_sum(c):
        wait(zr_ref.at[c], zz_r.at[c])
        ys_ref[c] = qs_ref[c, z] + zr_ref[c, 0] + zr_ref[c, 1] + zr_ref[c, 2]
        slot = lax.rem(y - c + NY - 1, NY)

        @pl.when(y != c)
        def _():
            send(ys_ref.at[c], yr_ref.at[slot], yy_s.at[c], yy_r, (c * NZ + z) * 2 + core, x)

    def key_send():
        to_heads(lambda r, o: send(
            ka_ref.at[pl.ds(pl.multiple_of(o * SQ, SQ), SQ)], kx_ref.at[r - 1], kx_s, kx_r, k, o))

    def key_sum():
        wait(kx_ref, kx_r)
        ko_ref[pl.ds(myq, SQ), :] = (
            ka_ref[pl.ds(myq, SQ), :] + kx_ref[0] + kx_ref[1] + kx_ref[2]
        ) * IS
        to_heads(lambda r, o: send(
            ko_ref.at[pl.ds(myq, SQ)], ko_ref.at[pl.ds(myq, SQ)], ko_s, ko_r, k, o))

    gw_ref[...] = jnp.zeros_like(gw_ref)
    ka_ref[...] = jnp.zeros_like(ka_ref)
    for c in range(C):
        index_forward(c)
    scores(0)
    logit_stats()
    scores(1)
    combine(0)
    logit_stats_heads()
    scores(2)
    combine(1)
    target(0)
    logit_stats_keys()
    scores(3)
    combine(2)
    logit_grad(0)
    target(1)
    grads(0)
    combine(3)
    logit_grad(1)
    target(2)
    pair_sum(0)
    grads(1)
    logit_grad(2)
    target(3)
    plane_sum(0)
    pair_sum(1)
    grads(2)
    logit_grad(3)
    plane_sum(1)
    pair_sum(2)
    grads(3)
    key_send()
    plane_sum(2)
    pair_sum(3)
    key_sum()
    plane_sum(3)
    wait(yr_ref, yy_r)
    mine = ys_ref[y] + yr_ref[0] + yr_ref[1] + yr_ref[2]
    oq_ref[...] = mine[:JL]
    ow_ref[...] = mine[JL]
    wait(kx_ref, ko_r)
    ok_ref[...] = ko_ref[...]

    wait(xr_ref, xs_s)
    wait(kr_ref, kk_s)
    wait(kx_ref, kx_s)
    wait(kx_ref, ko_s)
    for c in range(C):
        wait(lr_ref.at[c], lo_s.at[c])
        wait(sr_ref.at[c], ss_s.at[c])
        wait(sr_ref.at[c], gl_s.at[c])
        wait(tr_ref.at[c], tg_s.at[c])
        wait(tr_ref.at[c], lg_s.at[c])
        wait(pr_ref.at[c], pp_s.at[c])
        wait(zr_ref.at[c], zz_s.at[c])

        @pl.when(y != c)
        def _():
            wait(ys_ref.at[c], yy_s.at[c])


def finish(oq_ref, ow_ref, ok_ref, q_ref, w_ref, k_ref):
    for j in range(JL):
        q_ref[:, j, :] = oq_ref[j]
    w_ref[...] = ow_ref[:, :JL]
    k_ref[...] = ok_ref[...]


def per_device(main_query, latent_keys, index_query, index_keys, index_weights, query_limit):
    vm = pl.BlockSpec(memory_space=pltpu.VMEM)
    dma = pltpu.SemaphoreType.DMA
    oq, ow, ok = pl.pallas_call(
        kernel,
        out_shape=(
            jax.ShapeDtypeStruct((JL, 16, DI), F32),
            jax.ShapeDtypeStruct((16, DI), F32),
            jax.ShapeDtypeStruct((S, DI), F32),
        ),
        in_specs=[pl.BlockSpec(memory_space=pl.ANY)] * 4 + [vm] * 2,
        out_specs=(vm, vm, vm),
        scratch_shapes=[
            pltpu.VMEM((2, HL, DL, T), BF16),
            pltpu.VMEM((3, HL, S, T), F32),
            pltpu.VMEM((4, S, 2 * T), F32),
            pltpu.VMEM((2, 1, 2 * T), F32),
            pltpu.VMEM((C, S, T), F32),
            pltpu.VMEM((DI, S), BF16),
            pltpu.VMEM((JL, 1, C * T), F32),
            pltpu.VMEM((JL, 1, T), F32),
            pltpu.VMEM((DL, S), BF16),
            pltpu.VMEM((S, DL), BF16),
            pltpu.VMEM((C * T, JL, DI), BF16),
            pltpu.VMEM((T * JL, DI), F32),
            pltpu.VMEM((JL, C * T, DI), BF16),
            pltpu.VMEM((S, DI), BF16),
            pltpu.VMEM((S, 4 * T), BF16),
            pltpu.VMEM((S, 4 * T), BF16),
            pltpu.VMEM((C, S, T), F32),
            pltpu.VMEM((C, NX - 1, SQ, T), F32),
            pltpu.VMEM((C, SQ, T), F32),
            pltpu.VMEM((C, 2, T), F32),
            pltpu.VMEM((NX - 1, C, 2, T), F32),
            pltpu.VMEM((C, 2, T), F32),
            pltpu.VMEM((NK - 1, C, 2, T), F32),
            pltpu.VMEM((C, 2, T), F32),
            pltpu.VMEM((C, HL, 2, T), F32),
            pltpu.VMEM((C, NK - 1, 2, T), F32),
            pltpu.VMEM((C, 2, T), F32),
            pltpu.VMEM((C, HL, 2, T), F32),
            pltpu.VMEM((HL, T), F32),
            pltpu.VMEM((C, S, T), F32),
            pltpu.VMEM((C, NX - 1, SQ, T), F32),
            pltpu.VMEM((C, S, T), F32),
            pltpu.VMEM((DI, T), F32),
            pltpu.VMEM((S, DI), F32),
            pltpu.VMEM((C, 2, NZ, JL + 1, 16, DI), F32),
            pltpu.VMEM((C, NZ, JL + 1, 16, DI), F32),
            pltpu.VMEM((C, NZ, JL + 1, 16, DI), F32),
            pltpu.VMEM((C, NZ - 1, JL + 1, 16, DI), F32),
            pltpu.VMEM((C, JL + 1, 16, DI), F32),
            pltpu.VMEM((NY - 1, JL + 1, 16, DI), F32),
            pltpu.VMEM((NX - 1, SQ, DI), F32),
            pltpu.VMEM((S, DI), F32),
            dma((2,)), dma((3,)),
            dma((C,)), dma((C,)), dma, dma, dma, dma, dma((C,)), dma((C,)), dma((C,)), dma((C,)),
            dma((C,)), dma((C,)), dma((C,)), dma((C,)), dma((C,)), dma((C,)), dma((C,)), dma((C,)),
            dma((C,)), dma, dma, dma, dma, dma,
        ],
        compiler_params=pltpu.CompilerParams(
            collective_id=0, has_side_effects=True, vmem_limit_bytes=67043328
        ),
    )(
        jnp.transpose(main_query, (1, 2, 0)),
        latent_keys.T,
        index_query,
        index_keys,
        index_weights.T,
        query_limit.reshape(1, -1),
    )
    return pl.pallas_call(
        finish,
        out_shape=(
            jax.ShapeDtypeStruct((16, JL, DI), F32),
            jax.ShapeDtypeStruct((16, JL), F32),
            jax.ShapeDtypeStruct((S, DI), F32),
        ),
        in_specs=[vm] * 3,
        out_specs=(vm, vm, vm),
    )(oq, ow, ok)


def solution(mesh):
    in_specs = (
        P(None, "heads", None),
        P("keys", None),
        P(None, "heads", None),
        P("keys", None),
        P(None, "heads"),
        P(),
    )
    out_specs = (P("keys", "heads", None), P("keys", "heads"), P("keys", None))
    return jax.shard_map(
        per_device, mesh=mesh, in_specs=in_specs, out_specs=out_specs, check_vma=False
    )
```

```python
import functools

import jax
import jax.numpy as jnp
from jax import lax
from jax.experimental import pallas as pl
from jax.experimental.pallas import tpu as pltpu
from jax.sharding import PartitionSpec as P

H = 128
DL = 576
HI = 64
DI = 128
NK = 32
NX = 4
NY = 4
NZ = 4
C = 4
T = 128
S = 512
SQ = S // NX
U = 2 * C
JU = 8
HL = H // NX
JL = HI // NX
LOG2E = 1.4426950408889634
K2 = 2.0 * DL ** (-0.5) * LOG2E
IS = DI ** (-0.5)
HS = HI ** (-0.5)
NEG = -1e30
BIG = 3e38
MESH = pl.DeviceIdType.MESH
F32 = jnp.float32
BF16 = jnp.bfloat16


def twice(a):
    return jnp.concatenate([a, a], axis=1)


def kernel(
    q_hbm, kt_hbm, iq_hbm, ik_hbm, w_ref, lim_ref,
    oq_ref, ow_ref, ok_ref,
    qb, p_ref, s_ref, m_ref, cap_ref, ikt_ref, wj_ref,
    kt_ref, k_ref, iqr_ref, tmp_ref, iq_ref, ik_ref, ga_ref, gb_ref,
    lo_ref, l3_ref, lq_ref, ls_ref, xr_ref, lk_ref, kr_ref, lf_ref,
    st_ref, sz_ref, sa_ref, sy_ref, sb_ref, sp_ref, cc_ref,
    tg_ref, t3_ref, lg_ref, gw_ref, ka_ref,
    qp_ref, pr_ref, qs_ref, z3_ref, ys_ref, y3_ref, k3_ref, ko_ref,
    qsem, isem,
    xs_s, xs_r, kk_s, kk_r, sz_s, sz_r, sy_s, sy_r, sp_s, sp_r,
    l_s, l_r, t_s, t_r, a_s, a_r, k_s, k_r, b_s, b_r,
    pp_s, pp_r, z_s, z_r, y_s, y_r,
):
    k = lax.axis_index("keys")
    x = lax.axis_index("heads")
    core = lax.rem(k, 2)
    z = lax.rem(k // 2, NZ)
    y = k // (2 * NZ)
    sibling = k + 1 - 2 * core

    def rows_at(o):
        return pl.multiple_of(o * SQ, SQ)

    def zkey(r):
        return (y * NZ + lax.rem(z + r, NZ)) * 2 + core

    def ykey(r):
        return (lax.rem(y + r, NY) * NZ + z) * 2 + core

    myq = rows_at(x)

    def q_copy(c):
        return pltpu.make_async_copy(
            q_hbm.at[:, :, pl.ds(c * T, T)], qb.at[c % 2], qsem.at[c % 2]
        )

    def send(src, dst, ssem, rsem, kd, xd):
        pltpu.make_async_remote_copy(
            src_ref=src, dst_ref=dst, send_sem=ssem, recv_sem=rsem,
            device_id=(kd, xd), device_id_type=MESH,
        ).start()

    def wait(ref, sem):
        pltpu.make_async_copy(ref, ref, sem).wait()

    def to_keys(fn):
        def body(r, carry):
            fn(r, lax.rem(k + r, NK))
            return carry

        lax.fori_loop(1, NK, body, 0)

    def to_heads(fn):
        for r in range(1, NX):
            fn(r, lax.rem(x + r, NX))

    def reduce_send(own, three, ssem, rsem):
        to_heads(lambda r, o: send(own.at[pl.ds(rows_at(o), SQ)], three.at[r - 1], ssem, rsem, k, o))

    def reduce_sum(own, three, rsem):
        wait(three, rsem)
        return own[pl.ds(myq, SQ), :] + three[0] + three[1] + three[2]

    def gather_send(own, ssem, rsem):
        mine = own.at[pl.ds(myq, SQ)]
        to_heads(lambda r, o: send(mine, mine, ssem, rsem, k, o))

    loads = [
        pltpu.make_async_copy(a, b, isem.at[n])
        for n, (a, b) in enumerate(((iq_hbm, iqr_ref), (ik_hbm, ik_ref), (kt_hbm, kt_ref)))
    ]
    for load in loads:
        load.start()
    q_copy(0).start()
    barrier = pltpu.get_barrier_semaphore()
    to_keys(lambda r, o: pl.semaphore_signal(barrier, inc=1, device_id=(o, x), device_id_type=MESH))
    to_heads(lambda r, o: pl.semaphore_signal(barrier, inc=1, device_id=(k, o), device_id_type=MESH))

    pos = k * S + lax.broadcasted_iota(jnp.int32, (S, T), 0)
    for c in range(C):
        cap_ref[c] = jnp.where(pos <= lim_ref[0:1, c * T : (c + 1) * T], BIG, NEG)
    def prepare():
        for j in range(JL):
            wj_ref[j] = w_ref[j : j + 1, :]
        loads[1].wait()
        ikt_ref[...] = ik_ref[...].astype(F32).T.astype(BF16)
        loads[0].wait()
        for c in range(C):
            tmp_ref[...] = iqr_ref[c * T : (c + 1) * T].astype(F32).reshape(T * JL, DI)
            for j in range(JL):
                iq_ref[j, c * T : (c + 1) * T] = tmp_ref[pl.ds(j, T, stride=JL), :].astype(BF16)

    def prepare_keys():
        loads[2].wait()
        for b in range(S // 128):
            k_ref[b * 128 : (b + 1) * 128, :] = (
                kt_ref[:, b * 128 : (b + 1) * 128].astype(F32).T.astype(BF16)
            )

    def rows_of(c, jj):
        return jnp.concatenate(
            [wj_ref[2 * jj, :, c * T : (c + 1) * T], wj_ref[2 * jj + 1, :, c * T : (c + 1) * T]],
            axis=1,
        )

    def index_dots(c, jj, u):
        pair = iq_ref[pl.ds(2 * jj, 2), c * T : (c + 1) * T, :].reshape(2 * T, DI)
        s_ref[u] = lax.dot_general(
            ik_ref[...], pair, (((1,), (1,)), ((), ())), preferred_element_type=F32
        )

    def index_forward(c):
        lo_ref[c] = jnp.zeros((S, T), F32)

        def add(jj, u):
            total = None
            for v in range(2):
                row = rows_of(c, jj + v) * (IS * HS)
                term = jnp.maximum(s_ref[u + v], 0.0) * row
                part = term[:, :T] + term[:, T:]
                total = part if total is None else total + part
            lo_ref[c] += total

        def two(jj, u):
            index_dots(c, jj, u)
            index_dots(c, jj + 1, u + 1)

        two(0, 0)

        def body(i, carry):
            two(4 * i + 2, 2)
            add(4 * i, 0)
            two(jnp.minimum(4 * i + 4, JL // 2 - 2), 0)
            add(4 * i + 2, 2)
            return carry

        lax.fori_loop(0, JL // 8, body, 0)

    def logits_send(c):
        reduce_send(lo_ref.at[c], l3_ref.at[c], l_s.at[c], l_r.at[c])

    def scores(c, between):
        q_copy(c).wait()
        if c + 1 < C:
            q_copy(c + 1).start()
        slot = c % 2
        ps = c % 3

        def dots(i, u):
            h = 2 * i
            qt = jnp.concatenate([qb[slot, h], qb[slot, h + 1]], axis=1)
            s = jnp.dot(k_ref[...], qt, preferred_element_type=F32)
            s = jnp.minimum(s, twice(cap_ref[c]))
            s_ref[u] = s
            m = jnp.max(s, axis=0, keepdims=True)
            m_ref[u] = m
            st_ref[c, h, 0:1, :] = m[:, :T]
            st_ref[c, h + 1, 0:1, :] = m[:, T:]

        def soft(i, u):
            h = 2 * i
            p = jnp.exp2((s_ref[u] - m_ref[u]) * K2)
            l = jnp.sum(p, axis=0, keepdims=True)
            p_ref[ps, h] = p[:, :T]
            p_ref[ps, h + 1] = p[:, T:]
            st_ref[c, h, 1:2, :] = l[:, :T]
            st_ref[c, h + 1, 1:2, :] = l[:, T:]

        dots(0, 0)

        def body(i, carry):
            dots(2 * i + 1, 1)
            soft(2 * i, 0)
            dots(jnp.minimum(2 * i + 2, HL // 2 - 1), 0)
            soft(2 * i + 1, 1)
            return carry

        piece = HL // 4 // len(between)
        for n, action in enumerate(between):
            lax.fori_loop(n * piece, (n + 1) * piece, body, 0)
            action()
        for r in range(1, NZ):
            send(st_ref.at[c], sz_ref.at[c, r - 1], sz_s.at[c], sz_r.at[c], zkey(r), x)

    def merge(parts):
        ms = [p[:, 0, :] for p in parts]
        m = functools.reduce(jnp.maximum, ms)
        return m, sum(p[:, 1, :] * jnp.exp2((a - m) * K2) for a, p in zip(ms, parts))

    def stats_y(c):
        wait(sz_ref.at[c], sz_r.at[c])
        m, total = merge([st_ref[c]] + [sz_ref[c, r] for r in range(NZ - 1)])
        sa_ref[c, :, 0, :] = m
        sa_ref[c, :, 1, :] = total
        for r in range(1, NY):
            send(sa_ref.at[c], sy_ref.at[c, r - 1], sy_s.at[c], sy_r.at[c], ykey(r), x)

    def stats_core(c):
        wait(sy_ref.at[c], sy_r.at[c])
        m, total = merge([sa_ref[c]] + [sy_ref[c, r] for r in range(NY - 1)])
        sb_ref[c, :, 0, :] = m
        sb_ref[c, :, 1, :] = total
        send(sb_ref.at[c], sp_ref.at[c], sp_s.at[c], sp_r.at[c], sibling, x)

    def logit_stats():
        for c in range(C):
            v = reduce_sum(lo_ref.at[c], l3_ref.at[c], l_r.at[c])
            v = jnp.minimum(v, cap_ref[c, pl.ds(myq, SQ), :])
            lq_ref[c] = v
            m = jnp.max(v, axis=0, keepdims=True)
            ls_ref[c, 0:1, :] = m
            ls_ref[c, 1:2, :] = jnp.sum(jnp.exp(v - m), axis=0, keepdims=True)
        to_heads(lambda r, o: send(ls_ref, xr_ref.at[r - 1], xs_s, xs_r, k, o))

    def logit_stats_heads():
        wait(xr_ref, xs_r)
        for c in range(C):
            ms = [ls_ref[c, 0:1, :]] + [xr_ref[r, c, 0:1, :] for r in range(NX - 1)]
            ts = [ls_ref[c, 1:2, :]] + [xr_ref[r, c, 1:2, :] for r in range(NX - 1)]
            m = functools.reduce(jnp.maximum, ms)
            lk_ref[c, 0:1, :] = m
            lk_ref[c, 1:2, :] = sum(t * jnp.exp(a - m) for a, t in zip(ms, ts))
        to_keys(lambda r, o: send(lk_ref, kr_ref.at[r - 1], kk_s, kk_r, o, x))

    def logit_stats_keys():
        wait(kr_ref, kk_r)
        for c in range(C):
            own_m, own_t = lk_ref[c, 0:1, :], lk_ref[c, 1:2, :]
            ms = kr_ref[:, c, 0, :]
            ts = kr_ref[:, c, 1, :]
            m = jnp.maximum(own_m, jnp.max(ms, axis=0, keepdims=True))
            lf_ref[c, 0:1, :] = m
            lf_ref[c, 1:2, :] = own_t * jnp.exp(own_m - m) + jnp.sum(
                ts * jnp.exp(ms - m), axis=0, keepdims=True
            )

    def target(c):
        wait(sp_ref.at[c], sp_r.at[c])
        m, total = merge([sb_ref[c], sp_ref[c]])
        cc_ref[...] = jnp.exp2((st_ref[c, :, 0, :] - m) * K2) / (total * H)
        ps = c % 3
        rows = 64

        def body(b, carry):
            at = pl.ds(pl.multiple_of(b * rows, rows), rows)
            acc = p_ref[ps, 0, at, :] * cc_ref[0:1, :]
            for h in range(1, HL):
                acc += p_ref[ps, h, at, :] * cc_ref[h : h + 1, :]
            tg_ref[c, at, :] = acc
            return carry

        lax.fori_loop(0, S // rows, body, 0)
        reduce_send(tg_ref.at[c], t3_ref.at[c], t_s.at[c], t_r.at[c])

    def logit_grad(c):
        t = reduce_sum(tg_ref.at[c], t3_ref.at[c], t_r.at[c])
        v = lq_ref[c]
        probs = jnp.where(
            cap_ref[c, pl.ds(myq, SQ), :] > 0, jnp.exp(v - lf_ref[c, 0:1, :]), 0.0
        ) / lf_ref[c, 1:2, :]
        span = (lim_ref[0:1, c * T : (c + 1) * T] + 1).astype(F32)
        lg_ref[c, pl.ds(myq, SQ), :] = (probs - t) * span
        gather_send(lg_ref.at[c], a_s.at[c], a_r.at[c])

    def grads(c, half):
        unit = 2 * c + half
        base = JU * half
        if half == 0:
            wait(t3_ref.at[c], a_r.at[c])

        def gate(jj, u, out, at):
            dots = s_ref[u]
            lg = twice(lg_ref[c])
            gw = jnp.sum(lg * jnp.maximum(dots, 0.0), axis=0, keepdims=True) * (IS * HS)
            at_j = 2 * jj - base
            gw_ref[at_j : at_j + 1, :] = gw[:, :T]
            gw_ref[at_j + 1 : at_j + 2, :] = gw[:, T:]
            g = jnp.where(dots > 0, lg * (rows_of(c, jj) * HS), 0.0)
            out[:, at : at + 2 * T] = g.astype(BF16)

        def products(g_ref, j0):
            g = g_ref[...]
            four = iq_ref[j0 : j0 + 4, c * T : (c + 1) * T, :].reshape(4 * T, DI)
            qpt = jnp.dot(ikt_ref[...], g, preferred_element_type=F32) * IS
            for u in range(4):
                qp = qpt[:, u * T : (u + 1) * T].T
                for zz in range(NZ):
                    for cr in range(2):
                        at = (zz * 2 + cr) * 16
                        qp_ref[unit, cr, zz, j0 - base + u] = qp[at : at + 16]
            ka_ref[...] += jnp.dot(g, four, preferred_element_type=F32)

        first = base // 2
        index_dots(c, first, 0)
        for u in range(4):
            if u < 3:
                index_dots(c, first + u + 1, (u + 1) % 2)
            gate(first + u, u % 2, ga_ref if u < 2 else gb_ref, (u % 2) * 2 * T)
            if u == 1:
                products(ga_ref, base)
        products(gb_ref, base + 4)
        gwt = gw_ref[...].T
        for zz in range(NZ):
            for cr in range(2):
                at = (zz * 2 + cr) * 16
                qp_ref[unit, cr, zz, JU] = gwt[at : at + 16]
        send(
            qp_ref.at[unit, 1 - core], pr_ref.at[unit], pp_s.at[unit], pp_r.at[unit], sibling, x
        )

    def pair_sum(u):
        wait(pr_ref.at[u], pp_r.at[u])
        for zz in range(NZ):
            qs_ref[u, zz] = qp_ref[u, core, zz] + pr_ref[u, zz]
        for r in range(1, NZ):
            send(
                qs_ref.at[u, lax.rem(z + r, NZ)], z3_ref.at[u, r - 1], z_s.at[u], z_r.at[u], zkey(r), x
            )

    def plane_sum(u):
        wait(z3_ref.at[u], z_r.at[u])
        ys_ref[u] = qs_ref[u, z] + z3_ref[u, 0] + z3_ref[u, 1] + z3_ref[u, 2]
        away = lax.rem(y - u // 2 + NY, NY)

        @pl.when(away != 0)
        def _():
            send(ys_ref.at[u], y3_ref.at[u % 2, away - 1], y_s.at[u], y_r.at[u % 2], ykey(NY - away), x)

    def key_send():
        reduce_send(ka_ref, k3_ref, k_s, k_r)

    def key_sum():
        ko_ref[pl.ds(myq, SQ), :] = reduce_sum(ka_ref, k3_ref, k_r) * IS
        gather_send(ko_ref, b_s, b_r)

    gw_ref[...] = jnp.zeros_like(gw_ref)
    ka_ref[...] = jnp.zeros_like(ka_ref)

    def nothing():
        pass

    def sched(*steps):
        def run():
            for step, arg in steps:
                if arg is None:
                    step()
                else:
                    step(arg)

        return run

    def each(step, *units):
        for u in units:
            step(u)

    prepare()
    index_forward(0)
    index_forward(1)
    pl.semaphore_wait(barrier, NK - 1 + NX - 1)
    logits_send(0)
    logits_send(1)
    index_forward(2)
    logits_send(2)
    index_forward(3)
    logits_send(3)
    prepare_keys()
    scores(0, (nothing,))
    scores(1, (nothing, nothing, sched((stats_y, 0)), sched((logit_stats, None))))
    scores(2, (
        sched((stats_core, 0)), sched((target, 0), (logit_stats_heads, None)), sched((stats_y, 1)), nothing,
    ))
    scores(3, (
        sched((stats_core, 1)), sched((logit_stats_keys, None), (logit_grad, 0), (target, 1)),
        sched((stats_y, 2)), nothing,
    ))
    grads(0, 0)
    stats_core(2)
    logit_grad(1)
    target(2)
    grads(0, 1)
    stats_y(3)
    each(pair_sum, 0, 1)
    stats_core(3)
    grads(1, 0)
    logit_grad(2)
    target(3)
    grads(1, 1)
    each(pair_sum, 2, 3)
    each(plane_sum, 0, 1)
    grads(2, 0)
    grads(2, 1)
    logit_grad(3)
    each(pair_sum, 4, 5)
    each(plane_sum, 2, 3)
    grads(3, 0)
    grads(3, 1)
    key_send()
    each(pair_sum, 6, 7)
    each(plane_sum, 4, 5)
    key_sum()
    each(plane_sum, 6, 7)
    for half in range(2):
        wait(y3_ref.at[half], y_r.at[half])
        three = y3_ref.at[half]
        mine = ys_ref[2 * y + half] + three[0] + three[1] + three[2]
        oq_ref[half * JU : (half + 1) * JU] = mine[:JU]
        ow_ref[half] = mine[JU]
    wait(k3_ref, b_r)
    ok_ref[...] = ko_ref[...]

    wait(xr_ref, xs_s)
    wait(kr_ref, kk_s)
    wait(k3_ref, k_s)
    wait(k3_ref, b_s)
    for c in range(C):
        wait(l3_ref.at[c], l_s.at[c])
        wait(t3_ref.at[c], t_s.at[c])
        wait(t3_ref.at[c], a_s.at[c])
        wait(sz_ref.at[c], sz_s.at[c])
        wait(sy_ref.at[c], sy_s.at[c])
        wait(sp_ref.at[c], sp_s.at[c])
    for u in range(U):
        wait(pr_ref.at[u], pp_s.at[u])
        wait(z3_ref.at[u], z_s.at[u])

        @pl.when(y != u // 2)
        def _():
            wait(ys_ref.at[u], y_s.at[u])


def finish(oq_ref, ow_ref, ok_ref, q_ref, w_ref, k_ref):
    for j in range(JL):
        q_ref[:, j, :] = oq_ref[j]
    for half in range(2):
        w_ref[:, half * JU : (half + 1) * JU] = ow_ref[half, :, :JU]
    k_ref[...] = ok_ref[...]


def per_device(main_query, latent_keys, index_query, index_keys, index_weights, query_limit):
    vm = pl.BlockSpec(memory_space=pltpu.VMEM)
    dma = pltpu.SemaphoreType.DMA
    oq, ow, ok = pl.pallas_call(
        kernel,
        out_shape=(
            jax.ShapeDtypeStruct((JL, 16, DI), F32),
            jax.ShapeDtypeStruct((2, 16, DI), F32),
            jax.ShapeDtypeStruct((S, DI), F32),
        ),
        in_specs=[pl.BlockSpec(memory_space=pl.ANY)] * 4 + [vm] * 2,
        out_specs=(vm, vm, vm),
        scratch_shapes=[
            pltpu.VMEM((2, HL, DL, T), BF16),
            pltpu.VMEM((3, HL, S, T), F32),
            pltpu.VMEM((4, S, 2 * T), F32),
            pltpu.VMEM((2, 1, 2 * T), F32),
            pltpu.VMEM((C, S, T), F32),
            pltpu.VMEM((DI, S), BF16),
            pltpu.VMEM((JL, 1, C * T), F32),
            pltpu.VMEM((DL, S), BF16),
            pltpu.VMEM((S, DL), BF16),
            pltpu.VMEM((C * T, JL, DI), BF16),
            pltpu.VMEM((T * JL, DI), F32),
            pltpu.VMEM((JL, C * T, DI), BF16),
            pltpu.VMEM((S, DI), BF16),
            pltpu.VMEM((S, 4 * T), BF16),
            pltpu.VMEM((S, 4 * T), BF16),
            pltpu.VMEM((C, S, T), F32),
            pltpu.VMEM((C, NX - 1, SQ, T), F32),
            pltpu.VMEM((C, SQ, T), F32),
            pltpu.VMEM((C, 2, T), F32),
            pltpu.VMEM((NX - 1, C, 2, T), F32),
            pltpu.VMEM((C, 2, T), F32),
            pltpu.VMEM((NK - 1, C, 2, T), F32),
            pltpu.VMEM((C, 2, T), F32),
            pltpu.VMEM((C, HL, 2, T), F32),
            pltpu.VMEM((C, NZ - 1, HL, 2, T), F32),
            pltpu.VMEM((C, HL, 2, T), F32),
            pltpu.VMEM((C, NY - 1, HL, 2, T), F32),
            pltpu.VMEM((C, HL, 2, T), F32),
            pltpu.VMEM((C, HL, 2, T), F32),
            pltpu.VMEM((HL, T), F32),
            pltpu.VMEM((C, S, T), F32),
            pltpu.VMEM((C, NX - 1, SQ, T), F32),
            pltpu.VMEM((C, S, T), F32),
            pltpu.VMEM((DI, T), F32),
            pltpu.VMEM((S, DI), F32),
            pltpu.VMEM((U, 2, NZ, JU + 1, 16, DI), F32),
            pltpu.VMEM((U, NZ, JU + 1, 16, DI), F32),
            pltpu.VMEM((U, NZ, JU + 1, 16, DI), F32),
            pltpu.VMEM((U, NZ - 1, JU + 1, 16, DI), F32),
            pltpu.VMEM((U, JU + 1, 16, DI), F32),
            pltpu.VMEM((2, NY - 1, JU + 1, 16, DI), F32),
            pltpu.VMEM((NX - 1, SQ, DI), F32),
            pltpu.VMEM((S, DI), F32),
            dma((2,)), dma((3,)),
            dma, dma, dma, dma,
            *[dma((C,))] * 12, dma, dma, dma, dma,
            *[dma((U,))] * 5, dma((2,)),
        ],
        compiler_params=pltpu.CompilerParams(
            collective_id=0, has_side_effects=True, vmem_limit_bytes=67043328
        ),
    )(
        jnp.transpose(main_query, (1, 2, 0)),
        latent_keys.T,
        index_query,
        index_keys,
        index_weights.T,
        query_limit.reshape(1, -1),
    )
    return pl.pallas_call(
        finish,
        out_shape=(
            jax.ShapeDtypeStruct((16, JL, DI), F32),
            jax.ShapeDtypeStruct((16, JL), F32),
            jax.ShapeDtypeStruct((S, DI), F32),
        ),
        in_specs=[vm] * 3,
        out_specs=(vm, vm, vm),
    )(oq, ow, ok)


def solution(mesh):
    in_specs = (
        P(None, "heads", None),
        P("keys", None),
        P(None, "heads", None),
        P("keys", None),
        P(None, "heads"),
        P(),
    )
    out_specs = (P("keys", "heads", None), P("keys", "heads"), P("keys", None))
    return jax.shard_map(
        per_device, mesh=mesh, in_specs=in_specs, out_specs=out_specs, check_vma=False
    )
```

```python
import functools

import jax
import jax.numpy as jnp
from jax import lax
from jax.experimental import pallas as pl
from jax.experimental.pallas import tpu as pltpu
from jax.sharding import PartitionSpec as P

H = 128
DL = 576
HI = 64
DI = 128
NK = 32
NX = 4
NY = 4
NZ = 4
C = 4
T = 128
S = 512
SQ = S // NX
U = 2 * C
JU = 8
HL = H // NX
JL = HI // NX
LOG2E = 1.4426950408889634
K2 = 2.0 * DL ** (-0.5) * LOG2E
IS = DI ** (-0.5)
HS = HI ** (-0.5)
NEG = -1e30
BIG = 3e38
MESH = pl.DeviceIdType.MESH
F32 = jnp.float32
BF16 = jnp.bfloat16


def twice(a):
    return jnp.concatenate([a, a], axis=1)


def kernel(
    q_hbm, kt_hbm, iq_hbm, ik_hbm, w_ref, lim_ref,
    oq_ref, ow_ref, ok_ref,
    qb, p_ref, s_ref, m_ref, cap_ref, ikt_ref, wj_ref,
    kt_ref, k_ref, iqr_ref, tmp_ref, iq_ref, ik_ref, ga_ref, gb_ref,
    lo_ref, l3_ref, lq_ref, ls_ref, xr_ref, lk_ref, kr_ref, lf_ref,
    st_ref, sz_ref, sa_ref, sy_ref, sb_ref, sp_ref, cc_ref,
    tg_ref, t3_ref, lg_ref, gw_ref, ka_ref,
    qp_ref, pr_ref, qs_ref, z3_ref, ys_ref, y3_ref, k3_ref, ko_ref,
    qsem, isem,
    xs_s, xs_r, kk_s, kk_r, sz_s, sz_r, sy_s, sy_r, sp_s, sp_r,
    l_s, l_r, t_s, t_r, a_s, a_r, k_s, k_r, b_s, b_r,
    pp_s, pp_r, z_s, z_r, y_s, y_r,
):
    k = lax.axis_index("keys")
    x = lax.axis_index("heads")
    core = lax.rem(k, 2)
    z = lax.rem(k // 2, NZ)
    y = k // (2 * NZ)
    sibling = k + 1 - 2 * core

    def rows_at(o):
        return pl.multiple_of(o * SQ, SQ)

    def zkey(r):
        return (y * NZ + lax.rem(z + r, NZ)) * 2 + core

    def ykey(r):
        return (lax.rem(y + r, NY) * NZ + z) * 2 + core

    myq = rows_at(x)

    def q_copy(c):
        return pltpu.make_async_copy(
            q_hbm.at[:, :, pl.ds(c * T, T)], qb.at[c % 2], qsem.at[c % 2]
        )

    def send(src, dst, ssem, rsem, kd, xd):
        pltpu.make_async_remote_copy(
            src_ref=src, dst_ref=dst, send_sem=ssem, recv_sem=rsem,
            device_id=(kd, xd), device_id_type=MESH,
        ).start()

    def wait(ref, sem):
        pltpu.make_async_copy(ref, ref, sem).wait()

    def to_keys(fn):
        def body(r, carry):
            fn(r, lax.rem(k + r, NK))
            return carry

        lax.fori_loop(1, NK, body, 0)

    def to_heads(fn):
        for r in range(1, NX):
            fn(r, lax.rem(x + r, NX))

    def reduce_send(own, three, ssem, rsem):
        to_heads(lambda r, o: send(own.at[pl.ds(rows_at(o), SQ)], three.at[r - 1], ssem, rsem, k, o))

    def reduce_sum(own, three, rsem):
        wait(three, rsem)
        return own[pl.ds(myq, SQ), :] + three[0] + three[1] + three[2]

    def gather_send(own, ssem, rsem):
        mine = own.at[pl.ds(myq, SQ)]
        to_heads(lambda r, o: send(mine, mine, ssem, rsem, k, o))

    loads = [
        pltpu.make_async_copy(a, b, isem.at[n])
        for n, (a, b) in enumerate(((iq_hbm, iqr_ref), (ik_hbm, ik_ref), (kt_hbm, kt_ref)))
    ]
    for load in loads:
        load.start()
    q_copy(0).start()
    barrier = pltpu.get_barrier_semaphore()
    to_keys(lambda r, o: pl.semaphore_signal(barrier, inc=1, device_id=(o, x), device_id_type=MESH))
    to_heads(lambda r, o: pl.semaphore_signal(barrier, inc=1, device_id=(k, o), device_id_type=MESH))

    pos = k * S + lax.broadcasted_iota(jnp.int32, (S, T), 0)
    for c in range(C):
        cap_ref[c] = jnp.where(pos <= lim_ref[0:1, c * T : (c + 1) * T], BIG, NEG)
    def prepare():
        for j in range(JL):
            wj_ref[j] = w_ref[j : j + 1, :]
        loads[1].wait()
        ikt_ref[...] = ik_ref[...].astype(F32).T.astype(BF16)
        loads[0].wait()
        for c in range(C):
            tmp_ref[...] = iqr_ref[c * T : (c + 1) * T].astype(F32).reshape(T * JL, DI)
            for j in range(JL):
                iq_ref[j, c * T : (c + 1) * T] = tmp_ref[pl.ds(j, T, stride=JL), :].astype(BF16)

    def prepare_keys():
        loads[2].wait()
        for b in range(S // 128):
            k_ref[b * 128 : (b + 1) * 128, :] = (
                kt_ref[:, b * 128 : (b + 1) * 128].astype(F32).T.astype(BF16)
            )

    def rows_of(c, jj):
        return jnp.concatenate(
            [wj_ref[2 * jj, :, c * T : (c + 1) * T], wj_ref[2 * jj + 1, :, c * T : (c + 1) * T]],
            axis=1,
        )

    def index_dots(c, jj, u):
        pair = iq_ref[pl.ds(2 * jj, 2), c * T : (c + 1) * T, :].reshape(2 * T, DI)
        s_ref[u] = lax.dot_general(
            ik_ref[...], pair, (((1,), (1,)), ((), ())), preferred_element_type=F32
        )

    def index_forward(c):
        lo_ref[c] = jnp.zeros((S, T), F32)

        def add(jj, u):
            total = None
            for v in range(2):
                row = rows_of(c, jj + v) * (IS * HS)
                term = jnp.maximum(s_ref[u + v], 0.0) * row
                part = term[:, :T] + term[:, T:]
                total = part if total is None else total + part
            lo_ref[c] += total

        def two(jj, u):
            index_dots(c, jj, u)
            index_dots(c, jj + 1, u + 1)

        two(0, 0)

        def body(i, carry):
            two(4 * i + 2, 2)
            add(4 * i, 0)
            two(jnp.minimum(4 * i + 4, JL // 2 - 2), 0)
            add(4 * i + 2, 2)
            return carry

        lax.fori_loop(0, JL // 8, body, 0)

    def logits_send(c):
        reduce_send(lo_ref.at[c], l3_ref.at[c], l_s.at[c], l_r.at[c])

    def scores(c, between):
        q_copy(c).wait()
        if c + 1 < C:
            q_copy(c + 1).start()
        slot = c % 2
        ps = c % 3

        def dots(i, u):
            h = 2 * i
            qt = jnp.concatenate([qb[slot, h], qb[slot, h + 1]], axis=1)
            s = jnp.dot(k_ref[...], qt, preferred_element_type=F32)
            s = jnp.minimum(s, twice(cap_ref[c]))
            s_ref[u] = s
            m = jnp.max(s, axis=0, keepdims=True)
            m_ref[u] = m
            st_ref[c, h, 0:1, :] = m[:, :T]
            st_ref[c, h + 1, 0:1, :] = m[:, T:]

        def soft(i, u):
            h = 2 * i
            p = jnp.exp2((s_ref[u] - m_ref[u]) * K2)
            l = jnp.sum(p, axis=0, keepdims=True)
            p_ref[ps, h] = p[:, :T]
            p_ref[ps, h + 1] = p[:, T:]
            st_ref[c, h, 1:2, :] = l[:, :T]
            st_ref[c, h + 1, 1:2, :] = l[:, T:]

        dots(0, 0)

        def body(i, carry):
            dots(2 * i + 1, 1)
            soft(2 * i, 0)
            dots(jnp.minimum(2 * i + 2, HL // 2 - 1), 0)
            soft(2 * i + 1, 1)
            return carry

        piece = HL // 4 // len(between)
        for n, action in enumerate(between):
            lax.fori_loop(n * piece, (n + 1) * piece, body, 0)
            action()
        for r in range(1, NZ):
            send(st_ref.at[c], sz_ref.at[c, r - 1], sz_s.at[c], sz_r.at[c], zkey(r), x)

    def merge(parts):
        ms = [p[:, 0, :] for p in parts]
        m = functools.reduce(jnp.maximum, ms)
        return m, sum(p[:, 1, :] * jnp.exp2((a - m) * K2) for a, p in zip(ms, parts))

    def stats_y(c):
        wait(sz_ref.at[c], sz_r.at[c])
        m, total = merge([st_ref[c]] + [sz_ref[c, r] for r in range(NZ - 1)])
        sa_ref[c, :, 0, :] = m
        sa_ref[c, :, 1, :] = total
        for r in range(1, NY):
            send(sa_ref.at[c], sy_ref.at[c, r - 1], sy_s.at[c], sy_r.at[c], ykey(r), x)

    def stats_core(c):
        wait(sy_ref.at[c], sy_r.at[c])
        m, total = merge([sa_ref[c]] + [sy_ref[c, r] for r in range(NY - 1)])
        sb_ref[c, :, 0, :] = m
        sb_ref[c, :, 1, :] = total
        send(sb_ref.at[c], sp_ref.at[c], sp_s.at[c], sp_r.at[c], sibling, x)

    def logit_stats():
        for c in range(C):
            v = reduce_sum(lo_ref.at[c], l3_ref.at[c], l_r.at[c])
            v = jnp.minimum(v, cap_ref[c, pl.ds(myq, SQ), :])
            lq_ref[c] = v
            m = jnp.max(v, axis=0, keepdims=True)
            ls_ref[c, 0:1, :] = m
            ls_ref[c, 1:2, :] = jnp.sum(jnp.exp(v - m), axis=0, keepdims=True)
        to_heads(lambda r, o: send(ls_ref, xr_ref.at[r - 1], xs_s, xs_r, k, o))

    def logit_stats_heads():
        wait(xr_ref, xs_r)
        for c in range(C):
            ms = [ls_ref[c, 0:1, :]] + [xr_ref[r, c, 0:1, :] for r in range(NX - 1)]
            ts = [ls_ref[c, 1:2, :]] + [xr_ref[r, c, 1:2, :] for r in range(NX - 1)]
            m = functools.reduce(jnp.maximum, ms)
            lk_ref[c, 0:1, :] = m
            lk_ref[c, 1:2, :] = sum(t * jnp.exp(a - m) for a, t in zip(ms, ts))
        to_keys(lambda r, o: send(lk_ref, kr_ref.at[r - 1], kk_s, kk_r, o, x))

    def logit_stats_keys():
        wait(kr_ref, kk_r)
        for c in range(C):
            own_m, own_t = lk_ref[c, 0:1, :], lk_ref[c, 1:2, :]
            ms = kr_ref[:, c, 0, :]
            ts = kr_ref[:, c, 1, :]
            m = jnp.maximum(own_m, jnp.max(ms, axis=0, keepdims=True))
            lf_ref[c, 0:1, :] = m
            lf_ref[c, 1:2, :] = own_t * jnp.exp(own_m - m) + jnp.sum(
                ts * jnp.exp(ms - m), axis=0, keepdims=True
            )

    def target(c):
        wait(sp_ref.at[c], sp_r.at[c])
        m, total = merge([sb_ref[c], sp_ref[c]])
        cc_ref[...] = jnp.exp2((st_ref[c, :, 0, :] - m) * K2) / (total * H)
        ps = c % 3
        rows = 64

        def body(b, carry):
            at = pl.ds(pl.multiple_of(b * rows, rows), rows)
            acc = p_ref[ps, 0, at, :] * cc_ref[0:1, :]
            for h in range(1, HL):
                acc += p_ref[ps, h, at, :] * cc_ref[h : h + 1, :]
            tg_ref[c, at, :] = acc
            return carry

        lax.fori_loop(0, S // rows, body, 0)
        reduce_send(tg_ref.at[c], t3_ref.at[c], t_s.at[c], t_r.at[c])

    def logit_grad(c):
        t = reduce_sum(tg_ref.at[c], t3_ref.at[c], t_r.at[c])
        v = lq_ref[c]
        probs = jnp.where(
            cap_ref[c, pl.ds(myq, SQ), :] > 0, jnp.exp(v - lf_ref[c, 0:1, :]), 0.0
        ) / lf_ref[c, 1:2, :]
        span = (lim_ref[0:1, c * T : (c + 1) * T] + 1).astype(F32)
        lg_ref[c, pl.ds(myq, SQ), :] = (probs - t) * span
        gather_send(lg_ref.at[c], a_s.at[c], a_r.at[c])

    def grads(c, half):
        unit = 2 * c + half
        base = JU * half
        if half == 0:
            wait(t3_ref.at[c], a_r.at[c])

        def gate(jj, u, out, at):
            dots = s_ref[u]
            lg = twice(lg_ref[c])
            gw = jnp.sum(lg * jnp.maximum(dots, 0.0), axis=0, keepdims=True) * (IS * HS)
            at_j = 2 * jj - base
            gw_ref[at_j : at_j + 1, :] = gw[:, :T]
            gw_ref[at_j + 1 : at_j + 2, :] = gw[:, T:]
            g = jnp.where(dots > 0, lg * (rows_of(c, jj) * HS), 0.0)
            out[:, at : at + 2 * T] = g.astype(BF16)

        def products(g_ref, j0):
            g = g_ref[...]
            four = iq_ref[j0 : j0 + 4, c * T : (c + 1) * T, :].reshape(4 * T, DI)
            qpt = jnp.dot(ikt_ref[...], g, preferred_element_type=F32) * IS
            for u in range(4):
                qp = qpt[:, u * T : (u + 1) * T].T
                for zz in range(NZ):
                    for cr in range(2):
                        at = (zz * 2 + cr) * 16
                        qp_ref[unit, cr, zz, j0 - base + u] = qp[at : at + 16]
            ka_ref[...] += jnp.dot(g, four, preferred_element_type=F32)

        first = base // 2
        index_dots(c, first, 0)
        for u in range(4):
            if u < 3:
                index_dots(c, first + u + 1, (u + 1) % 2)
            gate(first + u, u % 2, ga_ref if u < 2 else gb_ref, (u % 2) * 2 * T)
            if u == 1:
                products(ga_ref, base)
        products(gb_ref, base + 4)
        gwt = gw_ref[...].T
        for zz in range(NZ):
            for cr in range(2):
                at = (zz * 2 + cr) * 16
                qp_ref[unit, cr, zz, JU] = gwt[at : at + 16]
        send(
            qp_ref.at[unit, 1 - core], pr_ref.at[unit], pp_s.at[unit], pp_r.at[unit], sibling, x
        )

    def pair_sum(u):
        wait(pr_ref.at[u], pp_r.at[u])
        for zz in range(NZ):
            qs_ref[u, zz] = qp_ref[u, core, zz] + pr_ref[u, zz]
        for r in range(1, NZ):
            send(
                qs_ref.at[u, lax.rem(z + r, NZ)], z3_ref.at[u, r - 1], z_s.at[u], z_r.at[u], zkey(r), x
            )

    def plane_sum(u):
        wait(z3_ref.at[u], z_r.at[u])
        ys_ref[u] = qs_ref[u, z] + z3_ref[u, 0] + z3_ref[u, 1] + z3_ref[u, 2]
        away = lax.rem(y - u // 2 + NY, NY)

        @pl.when(away != 0)
        def _():
            send(ys_ref.at[u], y3_ref.at[u % 2, away - 1], y_s.at[u], y_r.at[u % 2], ykey(NY - away), x)

    def key_send():
        reduce_send(ka_ref, k3_ref, k_s, k_r)

    def key_sum():
        ko_ref[pl.ds(myq, SQ), :] = reduce_sum(ka_ref, k3_ref, k_r) * IS
        gather_send(ko_ref, b_s, b_r)

    gw_ref[...] = jnp.zeros_like(gw_ref)
    ka_ref[...] = jnp.zeros_like(ka_ref)

    def nothing():
        pass

    def sched(*steps):
        def run():
            for step, arg in steps:
                if arg is None:
                    step()
                else:
                    step(arg)

        return run

    def each(step, *units):
        for u in units:
            step(u)

    prepare()
    index_forward(0)
    index_forward(1)
    pl.semaphore_wait(barrier, NK - 1 + NX - 1)
    logits_send(0)
    logits_send(1)
    index_forward(2)
    logits_send(2)
    index_forward(3)
    logits_send(3)
    prepare_keys()
    scores(0, (nothing,))
    scores(1, (nothing, nothing, sched((stats_y, 0)), sched((logit_stats, None))))
    scores(2, (
        nothing, sched((stats_core, 0), (logit_stats_heads, None)), sched((target, 0), (stats_y, 1)), nothing,
    ))
    scores(3, (
        sched((stats_core, 1)), sched((logit_stats_keys, None), (logit_grad, 0)),
        sched((stats_y, 2), (target, 1)), nothing,
    ))
    stats_core(2)
    grads(0, 0)
    stats_y(3)
    target(2)
    logit_grad(1)
    grads(0, 1)
    pair_sum(0)
    stats_core(3)
    pair_sum(1)
    target(3)
    logit_grad(2)
    grads(1, 0)
    grads(1, 1)
    each(plane_sum, 0, 1)
    each(pair_sum, 2, 3)
    logit_grad(3)
    grads(2, 0)
    grads(2, 1)
    each(pair_sum, 4, 5)
    each(plane_sum, 2, 3)
    grads(3, 0)
    grads(3, 1)
    key_send()
    each(pair_sum, 6, 7)
    each(plane_sum, 4, 5)
    key_sum()
    each(plane_sum, 6, 7)
    for half in range(2):
        wait(y3_ref.at[half], y_r.at[half])
        three = y3_ref.at[half]
        mine = ys_ref[2 * y + half] + three[0] + three[1] + three[2]
        oq_ref[half * JU : (half + 1) * JU] = mine[:JU]
        ow_ref[half] = mine[JU]
    wait(k3_ref, b_r)
    ok_ref[...] = ko_ref[...]

    wait(xr_ref, xs_s)
    wait(kr_ref, kk_s)
    wait(k3_ref, k_s)
    wait(k3_ref, b_s)
    for c in range(C):
        wait(l3_ref.at[c], l_s.at[c])
        wait(t3_ref.at[c], t_s.at[c])
        wait(t3_ref.at[c], a_s.at[c])
        wait(sz_ref.at[c], sz_s.at[c])
        wait(sy_ref.at[c], sy_s.at[c])
        wait(sp_ref.at[c], sp_s.at[c])
    for u in range(U):
        wait(pr_ref.at[u], pp_s.at[u])
        wait(z3_ref.at[u], z_s.at[u])

        @pl.when(y != u // 2)
        def _():
            wait(ys_ref.at[u], y_s.at[u])


def finish(oq_ref, ow_ref, ok_ref, q_ref, w_ref, k_ref):
    for j in range(JL):
        q_ref[:, j, :] = oq_ref[j]
    for half in range(2):
        w_ref[:, half * JU : (half + 1) * JU] = ow_ref[half, :, :JU]
    k_ref[...] = ok_ref[...]


def per_device(main_query, latent_keys, index_query, index_keys, index_weights, query_limit):
    vm = pl.BlockSpec(memory_space=pltpu.VMEM)
    dma = pltpu.SemaphoreType.DMA
    oq, ow, ok = pl.pallas_call(
        kernel,
        out_shape=(
            jax.ShapeDtypeStruct((JL, 16, DI), F32),
            jax.ShapeDtypeStruct((2, 16, DI), F32),
            jax.ShapeDtypeStruct((S, DI), F32),
        ),
        in_specs=[pl.BlockSpec(memory_space=pl.ANY)] * 4 + [vm] * 2,
        out_specs=(vm, vm, vm),
        scratch_shapes=[
            pltpu.VMEM((2, HL, DL, T), BF16),
            pltpu.VMEM((3, HL, S, T), F32),
            pltpu.VMEM((4, S, 2 * T), F32),
            pltpu.VMEM((2, 1, 2 * T), F32),
            pltpu.VMEM((C, S, T), F32),
            pltpu.VMEM((DI, S), BF16),
            pltpu.VMEM((JL, 1, C * T), F32),
            pltpu.VMEM((DL, S), BF16),
            pltpu.VMEM((S, DL), BF16),
            pltpu.VMEM((C * T, JL, DI), BF16),
            pltpu.VMEM((T * JL, DI), F32),
            pltpu.VMEM((JL, C * T, DI), BF16),
            pltpu.VMEM((S, DI), BF16),
            pltpu.VMEM((S, 4 * T), BF16),
            pltpu.VMEM((S, 4 * T), BF16),
            pltpu.VMEM((C, S, T), F32),
            pltpu.VMEM((C, NX - 1, SQ, T), F32),
            pltpu.VMEM((C, SQ, T), F32),
            pltpu.VMEM((C, 2, T), F32),
            pltpu.VMEM((NX - 1, C, 2, T), F32),
            pltpu.VMEM((C, 2, T), F32),
            pltpu.VMEM((NK - 1, C, 2, T), F32),
            pltpu.VMEM((C, 2, T), F32),
            pltpu.VMEM((C, HL, 2, T), F32),
            pltpu.VMEM((C, NZ - 1, HL, 2, T), F32),
            pltpu.VMEM((C, HL, 2, T), F32),
            pltpu.VMEM((C, NY - 1, HL, 2, T), F32),
            pltpu.VMEM((C, HL, 2, T), F32),
            pltpu.VMEM((C, HL, 2, T), F32),
            pltpu.VMEM((HL, T), F32),
            pltpu.VMEM((C, S, T), F32),
            pltpu.VMEM((C, NX - 1, SQ, T), F32),
            pltpu.VMEM((C, S, T), F32),
            pltpu.VMEM((DI, T), F32),
            pltpu.VMEM((S, DI), F32),
            pltpu.VMEM((U, 2, NZ, JU + 1, 16, DI), F32),
            pltpu.VMEM((U, NZ, JU + 1, 16, DI), F32),
            pltpu.VMEM((U, NZ, JU + 1, 16, DI), F32),
            pltpu.VMEM((U, NZ - 1, JU + 1, 16, DI), F32),
            pltpu.VMEM((U, JU + 1, 16, DI), F32),
            pltpu.VMEM((2, NY - 1, JU + 1, 16, DI), F32),
            pltpu.VMEM((NX - 1, SQ, DI), F32),
            pltpu.VMEM((S, DI), F32),
            dma((2,)), dma((3,)),
            dma, dma, dma, dma,
            *[dma((C,))] * 12, dma, dma, dma, dma,
            *[dma((U,))] * 5, dma((2,)),
        ],
        compiler_params=pltpu.CompilerParams(
            collective_id=0, has_side_effects=True, vmem_limit_bytes=67043328
        ),
    )(
        jnp.transpose(main_query, (1, 2, 0)),
        latent_keys.T,
        index_query,
        index_keys,
        index_weights.T,
        query_limit.reshape(1, -1),
    )
    return pl.pallas_call(
        finish,
        out_shape=(
            jax.ShapeDtypeStruct((16, JL, DI), F32),
            jax.ShapeDtypeStruct((16, JL), F32),
            jax.ShapeDtypeStruct((S, DI), F32),
        ),
        in_specs=[vm] * 3,
        out_specs=(vm, vm, vm),
    )(oq, ow, ok)


def solution(mesh):
    in_specs = (
        P(None, "heads", None),
        P("keys", None),
        P(None, "heads", None),
        P("keys", None),
        P(None, "heads"),
        P(),
    )
    out_specs = (P("keys", "heads", None), P("keys", "heads"), P("keys", None))
    return jax.shard_map(
        per_device, mesh=mesh, in_specs=in_specs, out_specs=out_specs, check_vma=False
    )
```
